256 devices in a mesh: seq: 32 (over z, y_lo, core), tensor: 8 (over x, y_hi).
Axes of the slice: x: 4, y: 4 (y_hi: 2, y_lo: 2; y = y_hi * 2 + y_lo), z: 8, core: 2. Of those that a mesh axis runs over, the one named last changes fastest.
Arguments:
- hidden_in: bfloat16 [8192, 8192], P('seq', 'tensor'), may hold values from -6 to 6
- frozen_query: bfloat16 [8192, 8192], P('seq', 'tensor'), may hold values from -48 to 48
- key_base: bfloat16 [8192, 1024], P('seq', 'tensor'), may hold values from -6 to 6
- frozen_value: bfloat16 [8192, 1024], P('seq', 'tensor'), may hold values from -6 to 6
- down_query: bfloat16 [8192, 16], P('tensor'), may hold values from -0.0625 to 0.0625
- query_upper_factor: bfloat16 [16, 8192], P(None, 'tensor'), may hold values from -1.5 to 1.5
- down_value: bfloat16 [8192, 16], P('tensor'), may hold values from -0.0625 to 0.0625
- value_upper_factor: bfloat16 [16, 1024], P(None, 'tensor'), may hold values from -1.5 to 1.5
- grad_output: bfloat16 [8192, 8192], P('seq', 'tensor'), may hold values from -6 to 6
Outputs:
- attention: bfloat16 [8192, 8192], P('seq', 'tensor')
- grad_down_query: float32 [8192, 16], P('tensor')
- gradient_query_upper: float32 [16, 8192], P(None, 'tensor')
- grad_down_value: float32 [8192, 16], P('tensor')
- gradient_value_upper: float32 [16, 1024], P(None, 'tensor')
The draws below stay inside these ranges and needn't reach their ends.
All inputs are finite; a program needn't handle non-finite values.
Results may differ from the reference program's by a relative error of at most 0.024.
Values may be sent and summed in bfloat16 or wider, within the bound.
A program may use at most 128 MiB of HBM per device.

```python
import jax
import jax.numpy as jnp
from jax import lax

D = 8192
H = 64
KV = 8
HD = 128
R = 16
GROUP = 2048
TOKENS = 8192


def draw_key_base(key, part):
    base_key = jax.random.fold_in(key, 7)
    result = jnp.clip(jax.random.normal(jax.random.fold_in(base_key, 2), (TOKENS, KV, HD)), -6.0, 6.0)
    return result.reshape(TOKENS, KV * HD).astype(jnp.bfloat16)


def draw_frozen_query(key, part):
    base_key = jax.random.fold_in(key, 7)
    result = jnp.clip(jax.random.normal(jax.random.fold_in(base_key, 5), (TOKENS, H, HD)), -6.0, 6.0)
    return result.reshape(TOKENS, H * HD).astype(jnp.bfloat16)


def level_of(stream_key, extent, shards, least, high):
    level = 1.0
    for axis_at, blocks in shards:
        draws = jax.random.uniform(jax.random.fold_in(jax.random.fold_in(stream_key, 6), axis_at), (blocks,), jnp.float32, least / len(shards), high / len(shards))
        level = level * jnp.repeat(jnp.exp(draws), extent[axis_at] // blocks).reshape((-1,) + (1,) * (len(extent) - 1 - axis_at))
    return level


def gaussian(rng, extent, width, limit, cuts=(), kind=jnp.bfloat16):
    factor_of = level_of(rng, extent, cuts, -0.22, 0.18) if cuts else 1.0
    values = jax.random.normal(rng, extent, jnp.float32) * width * factor_of
    return jnp.minimum(jnp.maximum(values, -limit), limit).astype(kind)


def setup_inputs(seed: int = 0) -> dict:
    seeds = jax.random.split(jax.random.key(seed), 10)
    hidden_in = gaussian(seeds[0], (TOKENS, D), 1.0, 6.0, ((0, 32), (1, 8)))
    frozen_query = draw_frozen_query(jax.random.fold_in(seeds[9], 71), 0)
    key_base = draw_key_base(jax.random.fold_in(seeds[9], 71), 0)
    frozen_value = gaussian(seeds[3], (TOKENS, KV * HD), 1.0, 6.0, ((0, 32), (1, 8)))
    down_query = gaussian(seeds[4], (D, R), D ** -0.5, 0.0625, ((0, 8),))
    query_upper_factor = gaussian(seeds[5], (R, H * HD), R ** -0.5, 1.5, ((1, 8),))
    down_value = gaussian(seeds[6], (D, R), D ** -0.5, 0.0625, ((0, 8),))
    value_upper_factor = gaussian(seeds[7], (R, KV * HD), R ** -0.5, 1.5, ((1, 8),))
    grad_output = gaussian(seeds[8], (TOKENS, H * HD), 1.0, 6.0, ((0, 32), (1, 8)))
    return {"hidden_in": hidden_in, "frozen_query": frozen_query, "key_base": key_base, "frozen_value": frozen_value, "down_query": down_query, "query_upper_factor": query_upper_factor, "down_value": down_value, "value_upper_factor": value_upper_factor, "grad_output": grad_output}


ADAPTER_SCALE = 0.5


def attend_group(inputs):
    query_matrix, keys, value_matrix, upstream = inputs
    scale_inv = float(HD) ** -0.5
    length = keys.shape[0]
    scores = jnp.einsum('tpd,sd->pts', query_matrix.astype(jnp.float32), keys.astype(jnp.float32)) * scale_inv
    causal = jnp.arange(length)[:, None] >= jnp.arange(length)[None, :]
    scores = jnp.where(causal, scores, -jnp.inf)
    row_max = jnp.max(scores, axis=-1, keepdims=True)
    lse = row_max + jnp.log(jnp.sum(jnp.exp(scores - row_max), axis=-1, keepdims=True))
    probs = jnp.exp(scores - lse)
    probs_bf = probs.astype(jnp.bfloat16)
    output = jnp.einsum('pts,sd->tpd', probs_bf.astype(jnp.float32), value_matrix.astype(jnp.float32)).astype(jnp.bfloat16)
    row_delta = jnp.sum(upstream.astype(jnp.float32) * output.astype(jnp.float32), axis=-1)
    grad_probs = jnp.einsum('tpd,sd->pts', upstream.astype(jnp.float32), value_matrix.astype(jnp.float32))
    grad_scores = (probs * (grad_probs - jnp.transpose(row_delta)[:, :, None]) * scale_inv).astype(jnp.bfloat16)
    grad_query = jnp.einsum('pts,sd->tpd', grad_scores.astype(jnp.float32), keys.astype(jnp.float32)).astype(jnp.bfloat16)
    grad_value = jnp.einsum('pts,tpd->sd', probs_bf.astype(jnp.float32), upstream.astype(jnp.float32)).astype(jnp.bfloat16)
    return output, grad_query, grad_value


def attend_head(inputs):
    head_index, query_matrix, keys, value_matrix, upstream = inputs
    per_head = H // KV
    shift_rows = jnp.where(head_index >= KV // 2, GROUP // 2, 0).astype(jnp.int32)
    groups = TOKENS // GROUP
    rolled_q = jnp.roll(query_matrix, -shift_rows, axis=0).reshape(groups, GROUP, per_head, HD)
    rolled_k = jnp.roll(keys, -shift_rows, axis=0).reshape(groups, GROUP, HD)
    rolled_v = jnp.roll(value_matrix, -shift_rows, axis=0).reshape(groups, GROUP, HD)
    rolled_g = jnp.roll(upstream, -shift_rows, axis=0).reshape(groups, GROUP, per_head, HD)
    output, grad_query, grad_value = lax.map(attend_group, (rolled_q, rolled_k, rolled_v, rolled_g))
    output = jnp.roll(output.reshape(TOKENS, per_head, HD), shift_rows, axis=0)
    grad_query = jnp.roll(grad_query.reshape(TOKENS, per_head, HD), shift_rows, axis=0)
    grad_value = jnp.roll(grad_value.reshape(TOKENS, HD), shift_rows, axis=0)
    return output, grad_query, grad_value


def reference(hidden_in, frozen_query, key_base, frozen_value, down_query, query_upper_factor, down_value, value_upper_factor, grad_output):
    per_head = H // KV
    reduced_query = jnp.dot(hidden_in, down_query, preferred_element_type=jnp.float32).astype(jnp.bfloat16)
    reduced_value = jnp.dot(hidden_in, down_value, preferred_element_type=jnp.float32).astype(jnp.bfloat16)
    query_matrix = (frozen_query.astype(jnp.float32) + ADAPTER_SCALE * jnp.dot(reduced_query, query_upper_factor, preferred_element_type=jnp.float32)).astype(jnp.bfloat16)
    value_matrix = (frozen_value.astype(jnp.float32) + ADAPTER_SCALE * jnp.dot(reduced_value, value_upper_factor, preferred_element_type=jnp.float32)).astype(jnp.bfloat16)
    head_q = jnp.transpose(query_matrix.reshape(TOKENS, KV, per_head, HD), (1, 0, 2, 3))
    head_k = jnp.transpose(key_base.reshape(TOKENS, KV, HD), (1, 0, 2))
    head_v = jnp.transpose(value_matrix.reshape(TOKENS, KV, HD), (1, 0, 2))
    head_g = jnp.transpose(grad_output.reshape(TOKENS, KV, per_head, HD), (1, 0, 2, 3))
    head_index = jnp.arange(KV, dtype=jnp.int32)
    output, grad_query, grad_value = lax.map(attend_head, (head_index, head_q, head_k, head_v, head_g))
    attention = jnp.transpose(output, (1, 0, 2, 3)).reshape(TOKENS, H * HD)
    query_gradient_rows = jnp.transpose(grad_query, (1, 0, 2, 3)).reshape(TOKENS, H * HD)
    value_gradient_rows = jnp.transpose(grad_value, (1, 0, 2)).reshape(TOKENS, KV * HD)
    gradient_query_upper = jnp.dot(reduced_query.T, query_gradient_rows, preferred_element_type=jnp.float32) * ADAPTER_SCALE
    gradient_value_upper = jnp.dot(reduced_value.T, value_gradient_rows, preferred_element_type=jnp.float32) * ADAPTER_SCALE
    restored_query = (ADAPTER_SCALE * jnp.dot(query_gradient_rows, query_upper_factor.T, preferred_element_type=jnp.float32)).astype(jnp.bfloat16)
    restored_value = (ADAPTER_SCALE * jnp.dot(value_gradient_rows, value_upper_factor.T, preferred_element_type=jnp.float32)).astype(jnp.bfloat16)
    grad_down_query = jnp.dot(hidden_in.T, restored_query, preferred_element_type=jnp.float32)
    grad_down_value = jnp.dot(hidden_in.T, restored_value, preferred_element_type=jnp.float32)
    return (attention, grad_down_query, gradient_query_upper, grad_down_value, gradient_value_upper)
```

```python
import jax
import jax.numpy as jnp
from jax import lax
from jax.experimental import pallas as pl
from jax.experimental.pallas import tpu as pltpu
from jax.sharding import PartitionSpec as P

HD = 128
GROUP = 2048
ADAPTER_SCALE = 0.5
MESH = pl.DeviceIdType.MESH
F32 = jnp.float32
BF16 = jnp.bfloat16
NT = (((1,), (1,)), ((), ()))
TN = (((0,), (0,)), ((), ()))


def mm(a, b, dims=(((1,), (0,)), ((), ()))):
    return lax.dot_general(a, b, dims, preferred_element_type=F32)


class Spot:
    def __init__(self, seq_count, tensor_count, members):
        self.seq_count, self.tensor_count, self.members = seq_count, tensor_count, members
        self.seq = lax.axis_index("seq")
        self.tensor = lax.axis_index("tensor")
        self.shift = jnp.where(self.tensor >= tensor_count // 2, members // 2, 0).astype(jnp.int32)
        frame = lax.rem(self.seq - self.shift + seq_count, seq_count)
        self.place = lax.rem(frame, members)
        self.base = frame - self.place + self.shift

    def member(self, place):
        return {"seq": lax.rem(self.base + place, self.seq_count), "tensor": self.tensor}

    def across(self, distance):
        return {"seq": self.seq, "tensor": lax.rem(self.tensor + distance, self.tensor_count)}

    def along(self, distance):
        return {"seq": lax.rem(self.seq + distance, self.seq_count), "tensor": self.tensor}


def remote(src, dst, send, recv, device):
    return pltpu.make_async_remote_copy(
        src_ref=src, dst_ref=dst, send_sem=send, recv_sem=recv, device_id=device, device_id_type=MESH
    )


def gather_kernel(
    sizes,
    hidden, down_q, down_v, keys, frozen_v,
    low_out, keys_out, values_out, lowv_out,
    part_slots, low_buf,
    part_send, part_recv, kv_send, kv_recv, low_send, low_recv, local_sem,
):
    spot = Spot(*sizes)
    members, count = spot.members, spot.tensor_count
    place, me = spot.place, spot.tensor
    barrier = pltpu.get_barrier_semaphore()
    for distance in range(1, count):
        pl.semaphore_signal(barrier, inc=1, device_id=spot.across(distance), device_id_type=MESH)
    for distance in range(1, members):
        pl.semaphore_signal(
            barrier, inc=1, device_id=spot.member(lax.rem(place + distance, members)), device_id_type=MESH
        )
    h = hidden[...]
    part_slots[me, 0:16, :] = mm(down_q[...], h, NT).astype(BF16)
    part_slots[me, 16:32, :] = mm(down_v[...], h, NT).astype(BF16)
    pl.semaphore_wait(barrier, count + members - 2)

    def part_copy(distance):
        return remote(
            part_slots.at[me], part_slots.at[me], part_send.at[distance], part_recv.at[me], spot.across(distance)
        )

    for distance in range(1, count):
        part_copy(distance).start()

    def kv_copies(distance):
        peer = spot.member(place + distance)
        return (
            remote(keys, keys_out.at[place], kv_send.at[0, distance], kv_recv.at[0, place], peer),
            remote(frozen_v, values_out.at[place], kv_send.at[1, distance], kv_recv.at[1, place], peer),
        )

    for distance in range(1, members):

        @pl.when(place + distance < members)
        def _():
            for copy in kv_copies(distance):
                copy.start()

    own_copies = (
        pltpu.make_async_copy(keys, keys_out.at[place], local_sem.at[0]),
        pltpu.make_async_copy(frozen_v, values_out.at[place], local_sem.at[1]),
    )
    for copy in own_copies:
        copy.start()
    for distance in range(1, count):
        source = lax.rem(me + distance, count)
        remote(
            part_slots.at[source], part_slots.at[source], part_send.at[0], part_recv.at[source], spot.across(distance)
        ).wait_recv()
    total = part_slots[0].astype(F32)
    for source in range(1, count):
        total = total + part_slots[source].astype(F32)
    low = total.astype(BF16)
    low_out[...] = low
    low_buf[...] = low[16:32]

    def low_copy(distance):
        return remote(
            low_buf, lowv_out.at[place], low_send.at[distance], low_recv.at[place], spot.member(place + distance)
        )

    for distance in range(1, members):

        @pl.when(place + distance < members)
        def _():
            low_copy(distance).start()

    own_low = pltpu.make_async_copy(low_buf, lowv_out.at[place], local_sem.at[2])
    own_low.start()
    for distance in range(1, members):

        @pl.when(place - distance >= 0)
        def _():
            source = place - distance
            peer = spot.member(source)
            remote(keys, keys_out.at[source], kv_send.at[0, 0], kv_recv.at[0, source], peer).wait_recv()
            remote(frozen_v, values_out.at[source], kv_send.at[1, 0], kv_recv.at[1, source], peer).wait_recv()
            remote(low_buf, lowv_out.at[source], low_send.at[0], low_recv.at[source], peer).wait_recv()

    for copy in own_copies:
        copy.wait()
    own_low.wait()
    for distance in range(1, count):
        part_copy(distance).wait_send()
    for distance in range(1, members):

        @pl.when(place + distance < members)
        def _():
            for copy in kv_copies(distance):
                copy.wait_send()
            low_copy(distance).wait_send()


def attention_kernel(
    sizes,
    low, keys, frozen_v, lowv, frozen_q, upper_q, upper_v, upstream,
    att, back_q, back_v, grad_uq, grad_uv,
    q_buf, v_buf, s_buf, p_buf, m_buf, l_buf, o_buf, dq_acc, dq_buf, dv_buf,
):
    spot = Spot(*sizes)
    place = spot.place
    rows = frozen_q.shape[0]
    heads = frozen_q.shape[1] // HD
    scale = float(HD) ** -0.5

    q_buf[...] = (frozen_q[...].astype(F32) + ADAPTER_SCALE * mm(low[0:16, :], upper_q[...], TN)).astype(BF16)

    def value_block(j, carry):
        v_buf[j] = (frozen_v[j].astype(F32) + ADAPTER_SCALE * mm(lowv[j], upper_v[...], TN)).astype(BF16)
        dv_buf[j] = jnp.zeros((HD, rows), F32)
        return carry

    lax.fori_loop(0, place + 1, value_block, 0)

    def span(j):
        return pl.ds(pl.multiple_of(j * rows, rows), rows)

    def wide(x):
        return jnp.concatenate((x,) * (rows // HD), axis=1)

    def halves(f, x):
        out = x[:, :HD]
        for at in range(HD, rows, HD):
            out = f(out, x[:, at : at + HD])
        return out

    def head(h, carry):
        cols = pl.ds(pl.multiple_of(h * HD, HD), HD)
        q = q_buf[:, cols]
        g = upstream[:, cols]
        s = mm(q, keys[place], NT)
        causal = lax.broadcasted_iota(jnp.int32, (rows, rows), 0) >= lax.broadcasted_iota(jnp.int32, (rows, rows), 1)
        s = jnp.where(causal, s, -jnp.inf)
        s_buf[:, span(place)] = s
        m_buf[...] = halves(jnp.maximum, s)

        def score(j, carry):
            s = mm(q, keys[j], NT)
            s_buf[:, span(j)] = s
            m_buf[...] = jnp.maximum(m_buf[...], halves(jnp.maximum, s))
            return carry

        lax.fori_loop(0, place, score, 0)
        m = jnp.broadcast_to(jnp.max(m_buf[...], axis=1, keepdims=True), (rows, HD))
        l_buf[...] = jnp.zeros((rows, HD), F32)
        o_buf[...] = jnp.zeros((rows, HD), F32)

        def weigh(j, carry):
            p = jnp.exp((s_buf[:, span(j)] - wide(m)) * scale)
            s_buf[:, span(j)] = p
            l_buf[...] += halves(jnp.add, p)
            pb = p.astype(BF16)
            p_buf[:, span(j)] = pb
            o_buf[...] += mm(pb, v_buf[j])
            return carry

        lax.fori_loop(0, place + 1, weigh, 0)
        inv = jnp.broadcast_to(1.0 / jnp.sum(l_buf[...], axis=1, keepdims=True), (rows, HD))
        o = (o_buf[...] * inv).astype(BF16)
        att[:, cols] = o
        gf = g.astype(F32)
        delta = jnp.broadcast_to(jnp.sum(gf * o.astype(F32), axis=1, keepdims=True), (rows, HD))
        gt = jnp.transpose((gf * inv).astype(BF16))
        weight = inv * scale
        dq_acc[...] = jnp.zeros((rows, HD), F32)

        def back(j, carry):
            dp = mm(g, v_buf[j], NT)
            ds = (s_buf[:, span(j)] * ((dp - wide(delta)) * wide(weight))).astype(BF16)
            dq_acc[...] += mm(ds, keys[j])
            dv_buf[j] += mm(gt, p_buf[:, span(j)])
            return carry

        lax.fori_loop(0, place + 1, back, 0)
        dq_buf[:, cols] = dq_acc[...].astype(BF16)
        return carry

    lax.fori_loop(0, heads, head, 0)
    dq = dq_buf[...]
    back_q[...] = mm(upper_q[...], dq, NT)
    grad_uq[...] = mm(low[0:16, :], dq) * ADAPTER_SCALE
    grad_uv[...] = jnp.zeros_like(grad_uv)
    back_v[...] = jnp.zeros_like(back_v)

    def value_back(j, carry):
        dv = dv_buf[j].astype(BF16)
        back_v[j] = mm(upper_v[...], dv).astype(BF16)
        grad_uv[...] += mm(lowv[j], dv, NT) * ADAPTER_SCALE
        return carry

    lax.fori_loop(0, place + 1, value_back, 0)


def reduce_kernel(
    sizes,
    hidden, back_q, back_v, grad_uq, grad_uv,
    down_q_out, down_v_out, upper_q_out, upper_v_out,
    group_slots, back_acc, part_slots, stage, sum_slots, result,
    group_send, group_recv, part_send, part_recv, sum_send, sum_recv, out_send, out_recv,
):
    spot = Spot(*sizes)
    members, count, seq_count = spot.members, spot.tensor_count, spot.seq_count
    place, me, seq = spot.place, spot.tensor, spot.seq
    chunks = stage.shape[0]
    barrier = pltpu.get_barrier_semaphore()
    for distance in range(1, count):
        pl.semaphore_signal(barrier, inc=1, device_id=spot.across(distance), device_id_type=MESH)

    def greet(distance, carry):
        pl.semaphore_signal(barrier, inc=1, device_id=spot.along(distance), device_id_type=MESH)
        return carry

    lax.fori_loop(1, seq_count, greet, 0)
    lanes = 128
    for at in range(8):
        stage[16 + at] = grad_uq[:, at * lanes : (at + 1) * lanes].astype(BF16)
    stage[24] = grad_uv[...].astype(BF16)
    pl.semaphore_wait(barrier, count + seq_count - 2)

    def group_copy(distance):
        target = place - distance
        return remote(
            back_v.at[target], group_slots.at[place], group_send.at[distance], group_recv.at[place], spot.member(target)
        )

    for distance in range(1, members):

        @pl.when(place - distance >= 0)
        def _():
            group_copy(distance).start()

    def sum_copy(chunk, distance):
        return remote(
            stage.at[chunk], sum_slots.at[seq], sum_send.at[distance], sum_recv.at[seq], spot.along(distance)
        )

    def send_chunks(first, last):
        def body(distance, carry):
            chunk = lax.rem(seq + distance, seq_count)

            @pl.when((chunk >= first) & (chunk < last))
            def _():
                sum_copy(chunk, distance).start()

            return carry

        lax.fori_loop(1, seq_count, body, 0)

    send_chunks(16, chunks)
    part_slots[me, 0:16, :] = back_q[...].astype(BF16)
    back_acc[...] = back_v[place].astype(F32)
    for distance in range(1, members):

        @pl.when(place + distance < members)
        def _():
            source = place + distance
            remote(
                back_v.at[place], group_slots.at[source], group_send.at[0], group_recv.at[source], spot.member(source)
            ).wait_recv()
            back_acc[...] += group_slots[source].astype(F32)

    part_slots[me, 16:32, :] = back_acc[...].astype(BF16)

    def part_copy(distance):
        return remote(
            part_slots.at[me], part_slots.at[me], part_send.at[distance], part_recv.at[me], spot.across(distance)
        )

    for distance in range(1, count):
        part_copy(distance).start()
    for distance in range(1, count):
        source = lax.rem(me + distance, count)
        remote(
            part_slots.at[source], part_slots.at[source], part_send.at[0], part_recv.at[source], spot.across(distance)
        ).wait_recv()
    total = part_slots[0].astype(F32)
    for source in range(1, count):
        total = total + part_slots[source].astype(F32)
    restored = (ADAPTER_SCALE * total).astype(BF16)
    grad_down = mm(restored, hidden[...])
    for at in range(8):
        stage[at] = grad_down[0:16, at * lanes : (at + 1) * lanes].astype(BF16)
        stage[8 + at] = grad_down[16:32, at * lanes : (at + 1) * lanes].astype(BF16)
    send_chunks(0, 16)

    def out_copy(distance):
        return remote(
            result.at[seq], result.at[seq], out_send.at[distance], out_recv.at[seq], spot.along(distance)
        )

    @pl.when(seq < chunks)
    def _():
        sum_slots[seq] = stage[seq]

        def arrive(distance, carry):
            source = lax.rem(seq + distance, seq_count)
            remote(
                stage.at[0], sum_slots.at[source], sum_send.at[0], sum_recv.at[source], spot.along(distance)
            ).wait_recv()
            return carry

        lax.fori_loop(1, seq_count, arrive, 0)

        def add(source, total):
            return total + sum_slots[source].astype(F32)

        result[seq] = lax.fori_loop(0, seq_count, add, jnp.zeros((16, lanes), F32)).astype(BF16)

        def send(distance, carry):
            out_copy(distance).start()
            return carry

        lax.fori_loop(1, seq_count, send, 0)

    def collect(distance, carry):
        source = lax.rem(seq + distance, seq_count)

        @pl.when(source < chunks)
        def _():
            remote(
                result.at[source], result.at[source], out_send.at[0], out_recv.at[source], spot.along(distance)
            ).wait_recv()

        return carry

    lax.fori_loop(1, seq_count, collect, 0)
    for at in range(8):
        cols = slice(at * lanes, (at + 1) * lanes)
        down_q_out[:, cols] = result[at].astype(F32)
        down_v_out[:, cols] = result[8 + at].astype(F32)
        upper_q_out[:, cols] = result[16 + at].astype(F32)
    upper_v_out[...] = result[24].astype(F32)

    for distance in range(1, members):

        @pl.when(place - distance >= 0)
        def _():
            group_copy(distance).wait_send()

    for distance in range(1, count):
        part_copy(distance).wait_send()

    def drain(distance, carry):
        chunk = lax.rem(seq + distance, seq_count)

        @pl.when(chunk < chunks)
        def _():
            sum_copy(chunk, distance).wait_send()

        @pl.when(seq < chunks)
        def _():
            out_copy(distance).wait_send()

        return carry

    lax.fori_loop(1, seq_count, drain, 0)


def per_device(
    hidden_in,
    frozen_query,
    key_base,
    frozen_value,
    down_query,
    query_upper_factor,
    down_value,
    value_upper_factor,
    grad_output,
):
    rows, width = hidden_in.shape
    rank = down_query.shape[1]
    seq_count, count = lax.axis_size("seq"), lax.axis_size("tensor")
    members = GROUP // rows
    sizes = (seq_count, count, members)
    chunks = 25
    vmem = pl.BlockSpec(memory_space=pltpu.VMEM)
    anywhere = pl.BlockSpec(memory_space=pl.ANY)
    dma = pltpu.SemaphoreType.DMA

    def shape(*dims, dtype=BF16):
        return jax.ShapeDtypeStruct(dims, dtype)

    low, keys, frozen_v, lowv = pl.pallas_call(
        lambda *refs: gather_kernel(sizes, *refs),
        out_shape=(
            shape(2 * rank, rows),
            shape(members, rows, HD),
            shape(members, rows, HD),
            shape(members, rank, rows),
        ),
        in_specs=[vmem] * 5,
        out_specs=(vmem, anywhere, anywhere, anywhere),
        scratch_shapes=[
            pltpu.VMEM((count, 2 * rank, rows), BF16),
            pltpu.VMEM((rank, rows), BF16),
            dma((count,)),
            dma((count,)),
            dma((2, members)),
            dma((2, members)),
            dma((members,)),
            dma((members,)),
            dma((3,)),
        ],
        compiler_params=pltpu.CompilerParams(collective_id=0, has_side_effects=True),
        name="gather",
    )(hidden_in, down_query.T, down_value.T, key_base, frozen_value)

    attention, back_q, back_v, grad_uq, grad_uv = pl.pallas_call(
        lambda *refs: attention_kernel(sizes, *refs),
        out_shape=(
            shape(rows, width),
            shape(rank, rows, dtype=F32),
            shape(members, rank, rows),
            shape(rank, width, dtype=F32),
            shape(rank, HD, dtype=F32),
        ),
        in_specs=[vmem] * 8,
        out_specs=(vmem,) * 5,
        scratch_shapes=[
            pltpu.VMEM((rows, width), BF16),
            pltpu.VMEM((members, rows, HD), BF16),
            pltpu.VMEM((rows, GROUP), F32),
            pltpu.VMEM((rows, GROUP), BF16),
            pltpu.VMEM((rows, HD), F32),
            pltpu.VMEM((rows, HD), F32),
            pltpu.VMEM((rows, HD), F32),
            pltpu.VMEM((rows, HD), F32),
            pltpu.VMEM((rows, width), BF16),
            pltpu.VMEM((members, HD, rows), F32),
        ],
        name="attention",
    )(low, keys, frozen_v, lowv, frozen_query, query_upper_factor, value_upper_factor, grad_output)

    down_q, down_v, upper_q, upper_v = pl.pallas_call(
        lambda *refs: reduce_kernel(sizes, *refs),
        out_shape=(
            shape(rank, width, dtype=F32),
            shape(rank, width, dtype=F32),
            shape(rank, width, dtype=F32),
            shape(rank, HD, dtype=F32),
        ),
        in_specs=[vmem] * 5,
        out_specs=(vmem,) * 4,
        scratch_shapes=[
            pltpu.VMEM((members, rank, rows), BF16),
            pltpu.VMEM((rank, rows), F32),
            pltpu.VMEM((count, 2 * rank, rows), BF16),
            pltpu.VMEM((chunks, rank, 128), BF16),
            pltpu.VMEM((seq_count, rank, 128), BF16),
            pltpu.VMEM((chunks, rank, 128), BF16),
            dma((members,)),
            dma((members,)),
            dma((count,)),
            dma((count,)),
            dma((seq_count,)),
            dma((seq_count,)),
            dma((seq_count,)),
            dma((seq_count,)),
        ],
        compiler_params=pltpu.CompilerParams(collective_id=1, has_side_effects=True),
        name="reduce",
    )(hidden_in, back_q, back_v, grad_uq, grad_uv)
    return (attention, down_q.T, upper_q, down_v.T, upper_v)


def solution(mesh):
    placed = (
        P("seq", "tensor"),
        P("seq", "tensor"),
        P("seq", "tensor"),
        P("seq", "tensor"),
        P("tensor", None),
        P(None, "tensor"),
        P("tensor", None),
        P(None, "tensor"),
        P("seq", "tensor"),
    )
    return jax.shard_map(
        per_device,
        mesh=mesh,
        in_specs=placed,
        out_specs=(
            P("seq", "tensor"),
            P("tensor", None),
            P(None, "tensor"),
            P("tensor", None),
            P(None, "tensor"),
        ),
        check_vma=False,
    )
```

```python
import jax
import jax.numpy as jnp
from jax import lax
from jax.experimental import pallas as pl
from jax.experimental.pallas import tpu as pltpu
from jax.sharding import PartitionSpec as P

HD = 128
GROUP = 2048
ADAPTER_SCALE = 0.5
MESH = pl.DeviceIdType.MESH
F32 = jnp.float32
BF16 = jnp.bfloat16
NT = (((1,), (1,)), ((), ()))
TN = (((0,), (0,)), ((), ()))


def mm(a, b, dims=(((1,), (0,)), ((), ()))):
    return lax.dot_general(a, b, dims, preferred_element_type=F32)


class Spot:
    def __init__(self, seq_count, tensor_count, members):
        self.seq_count, self.tensor_count, self.members = seq_count, tensor_count, members
        self.seq = lax.axis_index("seq")
        self.tensor = lax.axis_index("tensor")
        self.shift = jnp.where(self.tensor >= tensor_count // 2, members // 2, 0).astype(jnp.int32)
        frame = lax.rem(self.seq - self.shift + seq_count, seq_count)
        self.place = lax.rem(frame, members)
        self.base = frame - self.place + self.shift

    def member(self, place):
        return {"seq": lax.rem(self.base + place, self.seq_count), "tensor": self.tensor}

    def across(self, distance):
        return {"seq": self.seq, "tensor": lax.rem(self.tensor + distance, self.tensor_count)}

    def along(self, distance):
        return {"seq": lax.rem(self.seq + distance, self.seq_count), "tensor": self.tensor}


def remote(src, dst, send, recv, device):
    return pltpu.make_async_remote_copy(
        src_ref=src, dst_ref=dst, send_sem=send, recv_sem=recv, device_id=device, device_id_type=MESH
    )


def gather_kernel(
    sizes,
    hidden, down_q, down_v, keys, frozen_v,
    low_out, keys_out, values_out, lowv_out,
    part_slots, low_buf,
    part_send, part_recv, kv_send, kv_recv, low_send, low_recv, local_sem,
):
    spot = Spot(*sizes)
    members, count = spot.members, spot.tensor_count
    place, me = spot.place, spot.tensor
    barrier = pltpu.get_barrier_semaphore()
    for distance in range(1, count):
        pl.semaphore_signal(barrier, inc=1, device_id=spot.across(distance), device_id_type=MESH)
    for distance in range(1, members):
        pl.semaphore_signal(
            barrier, inc=1, device_id=spot.member(lax.rem(place + distance, members)), device_id_type=MESH
        )
    h = hidden[...]
    part_slots[me, 0:16, :] = mm(down_q[...], h, NT).astype(BF16)
    part_slots[me, 16:32, :] = mm(down_v[...], h, NT).astype(BF16)
    pl.semaphore_wait(barrier, count + members - 2)

    def part_copy(distance):
        return remote(
            part_slots.at[me], part_slots.at[me], part_send.at[distance], part_recv.at[me], spot.across(distance)
        )

    for distance in range(1, count):
        part_copy(distance).start()

    def kv_copies(distance):
        peer = spot.member(place + distance)
        return (
            remote(keys, keys_out.at[place], kv_send.at[0, distance], kv_recv.at[0, place], peer),
            remote(frozen_v, values_out.at[place], kv_send.at[1, distance], kv_recv.at[1, place], peer),
        )

    for distance in range(1, members):

        @pl.when(place + distance < members)
        def _():
            for copy in kv_copies(distance):
                copy.start()

    own_copies = (
        pltpu.make_async_copy(keys, keys_out.at[place], local_sem.at[0]),
        pltpu.make_async_copy(frozen_v, values_out.at[place], local_sem.at[1]),
    )
    for copy in own_copies:
        copy.start()
    for distance in range(1, count):
        source = lax.rem(me + distance, count)
        remote(
            part_slots.at[source], part_slots.at[source], part_send.at[0], part_recv.at[source], spot.across(distance)
        ).wait_recv()
    total = part_slots[0].astype(F32)
    for source in range(1, count):
        total = total + part_slots[source].astype(F32)
    low = total.astype(BF16)
    low_out[...] = low
    low_buf[...] = low[16:32]

    def low_copy(distance):
        return remote(
            low_buf, lowv_out.at[place], low_send.at[distance], low_recv.at[place], spot.member(place + distance)
        )

    for distance in range(1, members):

        @pl.when(place + distance < members)
        def _():
            low_copy(distance).start()

    own_low = pltpu.make_async_copy(low_buf, lowv_out.at[place], local_sem.at[2])
    own_low.start()
    for distance in range(1, members):

        @pl.when(place - distance >= 0)
        def _():
            source = place - distance
            peer = spot.member(source)
            remote(keys, keys_out.at[source], kv_send.at[0, 0], kv_recv.at[0, source], peer).wait_recv()
            remote(frozen_v, values_out.at[source], kv_send.at[1, 0], kv_recv.at[1, source], peer).wait_recv()
            remote(low_buf, lowv_out.at[source], low_send.at[0], low_recv.at[source], peer).wait_recv()

    for copy in own_copies:
        copy.wait()
    own_low.wait()
    for distance in range(1, count):
        part_copy(distance).wait_send()
    for distance in range(1, members):

        @pl.when(place + distance < members)
        def _():
            for copy in kv_copies(distance):
                copy.wait_send()
            low_copy(distance).wait_send()


def attention_kernel(
    sizes,
    low, keys, frozen_v, lowv, frozen_q, upper_q, upper_v, upstream,
    att, back_q, back_v, grad_uq, grad_uv,
    q_buf, g_buf, v_buf, s_buf, p_buf, m_buf, l_buf, o_buf, dq_buf, gt_buf, dv_buf,
):
    place = Spot(*sizes).place
    rows = frozen_q.shape[0]
    heads = frozen_q.shape[1] // HD
    rank = upper_q.shape[0]
    scale = float(HD) ** -0.5
    gain = scale * 1.4426950408889634

    def part(h):
        return slice(h * rows, (h + 1) * rows)

    def span(j):
        return pl.ds(pl.multiple_of(j * rows, rows), rows)

    def wide(x):
        return jnp.concatenate((x,) * (rows // HD), axis=1)

    def halves(f, x):
        out = x[:, :HD]
        for at in range(HD, rows, HD):
            out = f(out, x[:, at : at + HD])
        return out

    def row(f, x):
        return jnp.broadcast_to(f(x, axis=1, keepdims=True), (rows, HD))

    q = (frozen_q[...].astype(F32) + ADAPTER_SCALE * mm(low[0:rank, :], upper_q[...], TN)).astype(BF16)
    for h in range(heads):
        q_buf[part(h), :] = q[:, h * HD : (h + 1) * HD]

    def value_block(j, carry):
        v_buf[j] = (frozen_v[j].astype(F32) + ADAPTER_SCALE * mm(lowv[j], upper_v[...], TN)).astype(BF16)
        return carry

    lax.fori_loop(0, place + 1, value_block, 0)
    causal = lax.broadcasted_iota(jnp.int32, (rows, rows), 0) >= lax.broadcasted_iota(jnp.int32, (rows, rows), 1)
    for h in range(heads):
        s = jnp.where(causal, mm(q_buf[part(h), :], keys[place], NT), -jnp.inf)
        s_buf[part(h), span(place)] = s
        m_buf[part(h), :] = halves(jnp.maximum, s)

    def score(j, carry):
        for h in range(heads):
            s = mm(q_buf[part(h), :], keys[j], NT)
            s_buf[part(h), span(j)] = s
            m_buf[part(h), :] = jnp.maximum(m_buf[part(h), :], halves(jnp.maximum, s))
        return carry

    lax.fori_loop(0, place, score, 0)
    for h in range(heads):
        m_buf[part(h), :] = row(jnp.max, m_buf[part(h), :])
        l_buf[part(h), :] = jnp.zeros((rows, HD), F32)
        o_buf[part(h), :] = jnp.zeros((rows, HD), F32)
        dq_buf[part(h), :] = jnp.zeros((rows, HD), F32)

    def weigh(j, carry):
        for h in range(heads):
            p = jnp.exp2((s_buf[part(h), span(j)] - wide(m_buf[part(h), :])) * gain)
            s_buf[part(h), span(j)] = p
            l_buf[part(h), :] += halves(jnp.add, p)
            pb = p.astype(BF16)
            p_buf[part(h), span(j)] = pb
            o_buf[part(h), :] += mm(pb, v_buf[j])
        return carry

    lax.fori_loop(0, place + 1, weigh, 0)
    for h in range(heads):
        cols = slice(h * HD, (h + 1) * HD)
        inv = 1.0 / row(jnp.sum, l_buf[part(h), :])
        o = (o_buf[part(h), :] * inv).astype(BF16)
        att[:, cols] = o
        g = (upstream[:, cols].astype(F32) * inv).astype(BF16)
        g_buf[part(h), :] = g
        gt_buf[:, part(h)] = jnp.transpose(g)
        m_buf[part(h), :] = row(jnp.sum, g.astype(F32) * o.astype(F32))

    def back(j, carry):
        for h in range(heads):
            dp = mm(g_buf[part(h), :], v_buf[j], NT)
            ds = (s_buf[part(h), span(j)] * (dp - wide(m_buf[part(h), :]))).astype(BF16)
            dq_buf[part(h), :] += mm(ds, keys[j])
        dv_buf[j] = mm(gt_buf[...], p_buf[:, span(j)]).astype(BF16)
        return carry

    lax.fori_loop(0, place + 1, back, 0)
    dq = jnp.concatenate([(dq_buf[part(h), :] * scale).astype(BF16) for h in range(heads)], axis=1)
    back_q[...] = mm(upper_q[...], dq, NT)
    grad_uq[...] = mm(low[0:rank, :], dq) * ADAPTER_SCALE
    grad_uv[...] = jnp.zeros_like(grad_uv)
    back_v[...] = jnp.zeros_like(back_v)

    def value_back(j, carry):
        dv = dv_buf[j]
        back_v[j] = mm(upper_v[...], dv).astype(BF16)
        grad_uv[...] += mm(lowv[j], dv, NT) * ADAPTER_SCALE
        return carry

    lax.fori_loop(0, place + 1, value_back, 0)


def reduce_kernel(
    sizes,
    hidden, back_q, back_v, grad_uq, grad_uv,
    down_q_out, down_v_out, upper_q_out, upper_v_out,
    group_slots, back_acc, part_slots, stage, sum_slots, result,
    group_send, group_recv, part_send, part_recv, sum_send, sum_recv, out_send, out_recv,
):
    spot = Spot(*sizes)
    members, count, seq_count = spot.members, spot.tensor_count, spot.seq_count
    place, me, seq = spot.place, spot.tensor, spot.seq
    chunks = stage.shape[0]
    barrier = pltpu.get_barrier_semaphore()
    for distance in range(1, count):
        pl.semaphore_signal(barrier, inc=1, device_id=spot.across(distance), device_id_type=MESH)

    def greet(distance, carry):
        pl.semaphore_signal(barrier, inc=1, device_id=spot.along(distance), device_id_type=MESH)
        return carry

    lax.fori_loop(1, seq_count, greet, 0)
    lanes = 128
    for at in range(8):
        stage[16 + at] = grad_uq[:, at * lanes : (at + 1) * lanes].astype(BF16)
    stage[24] = grad_uv[...].astype(BF16)
    pl.semaphore_wait(barrier, count + seq_count - 2)

    def group_copy(distance):
        target = place - distance
        return remote(
            back_v.at[target], group_slots.at[place], group_send.at[distance], group_recv.at[place], spot.member(target)
        )

    for distance in range(1, members):

        @pl.when(place - distance >= 0)
        def _():
            group_copy(distance).start()

    def sum_copy(chunk, distance):
        return remote(
            stage.at[chunk], sum_slots.at[seq], sum_send.at[distance], sum_recv.at[seq], spot.along(distance)
        )

    def send_chunks(first, last):
        def body(distance, carry):
            chunk = lax.rem(seq + distance, seq_count)

            @pl.when((chunk >= first) & (chunk < last))
            def _():
                sum_copy(chunk, distance).start()

            return carry

        lax.fori_loop(1, seq_count, body, 0)

    send_chunks(16, chunks)
    part_slots[me, 0:16, :] = back_q[...].astype(BF16)
    back_acc[...] = back_v[place].astype(F32)
    for distance in range(1, members):

        @pl.when(place + distance < members)
        def _():
            source = place + distance
            remote(
                back_v.at[place], group_slots.at[source], group_send.at[0], group_recv.at[source], spot.member(source)
            ).wait_recv()
            back_acc[...] += group_slots[source].astype(F32)

    part_slots[me, 16:32, :] = back_acc[...].astype(BF16)

    def part_copy(distance):
        return remote(
            part_slots.at[me], part_slots.at[me], part_send.at[distance], part_recv.at[me], spot.across(distance)
        )

    for distance in range(1, count):
        part_copy(distance).start()
    for distance in range(1, count):
        source = lax.rem(me + distance, count)
        remote(
            part_slots.at[source], part_slots.at[source], part_send.at[0], part_recv.at[source], spot.across(distance)
        ).wait_recv()
    total = part_slots[0].astype(F32)
    for source in range(1, count):
        total = total + part_slots[source].astype(F32)
    restored = (ADAPTER_SCALE * total).astype(BF16)
    grad_down = mm(restored, hidden[...])
    for at in range(8):
        stage[at] = grad_down[0:16, at * lanes : (at + 1) * lanes].astype(BF16)
        stage[8 + at] = grad_down[16:32, at * lanes : (at + 1) * lanes].astype(BF16)
    send_chunks(0, 16)

    def out_copy(distance):
        return remote(
            result.at[seq], result.at[seq], out_send.at[distance], out_recv.at[seq], spot.along(distance)
        )

    @pl.when(seq < chunks)
    def _():
        sum_slots[seq] = stage[seq]

        def arrive(distance, carry):
            source = lax.rem(seq + distance, seq_count)
            remote(
                stage.at[0], sum_slots.at[source], sum_send.at[0], sum_recv.at[source], spot.along(distance)
            ).wait_recv()
            return carry

        lax.fori_loop(1, seq_count, arrive, 0)

        def add(source, total):
            return total + sum_slots[source].astype(F32)

        result[seq] = lax.fori_loop(0, seq_count, add, jnp.zeros((16, lanes), F32)).astype(BF16)

        def send(distance, carry):
            out_copy(distance).start()
            return carry

        lax.fori_loop(1, seq_count, send, 0)

    def collect(distance, carry):
        source = lax.rem(seq + distance, seq_count)

        @pl.when(source < chunks)
        def _():
            remote(
                result.at[source], result.at[source], out_send.at[0], out_recv.at[source], spot.along(distance)
            ).wait_recv()

        return carry

    lax.fori_loop(1, seq_count, collect, 0)
    for at in range(8):
        cols = slice(at * lanes, (at + 1) * lanes)
        down_q_out[:, cols] = result[at].astype(F32)
        down_v_out[:, cols] = result[8 + at].astype(F32)
        upper_q_out[:, cols] = result[16 + at].astype(F32)
    upper_v_out[...] = result[24].astype(F32)

    for distance in range(1, members):

        @pl.when(place - distance >= 0)
        def _():
            group_copy(distance).wait_send()

    for distance in range(1, count):
        part_copy(distance).wait_send()

    def drain(distance, carry):
        chunk = lax.rem(seq + distance, seq_count)

        @pl.when(chunk < chunks)
        def _():
            sum_copy(chunk, distance).wait_send()

        @pl.when(seq < chunks)
        def _():
            out_copy(distance).wait_send()

        return carry

    lax.fori_loop(1, seq_count, drain, 0)


def per_device(
    hidden_in,
    frozen_query,
    key_base,
    frozen_value,
    down_query,
    query_upper_factor,
    down_value,
    value_upper_factor,
    grad_output,
):
    rows, width = hidden_in.shape
    rank = down_query.shape[1]
    heads = frozen_query.shape[1] // HD
    seq_count, count = lax.axis_size("seq"), lax.axis_size("tensor")
    members = GROUP // rows
    sizes = (seq_count, count, members)
    chunks = 25
    vmem = pl.BlockSpec(memory_space=pltpu.VMEM)
    anywhere = pl.BlockSpec(memory_space=pl.ANY)
    dma = pltpu.SemaphoreType.DMA

    def shape(*dims, dtype=BF16):
        return jax.ShapeDtypeStruct(dims, dtype)

    low, keys, frozen_v, lowv = pl.pallas_call(
        lambda *refs: gather_kernel(sizes, *refs),
        out_shape=(
            shape(2 * rank, rows),
            shape(members, rows, HD),
            shape(members, rows, HD),
            shape(members, rank, rows),
        ),
        in_specs=[vmem] * 5,
        out_specs=(vmem, anywhere, anywhere, anywhere),
        scratch_shapes=[
            pltpu.VMEM((count, 2 * rank, rows), BF16),
            pltpu.VMEM((rank, rows), BF16),
            dma((count,)),
            dma((count,)),
            dma((2, members)),
            dma((2, members)),
            dma((members,)),
            dma((members,)),
            dma((3,)),
        ],
        compiler_params=pltpu.CompilerParams(collective_id=0, has_side_effects=True),
        name="gather",
    )(hidden_in, down_query.T, down_value.T, key_base, frozen_value)

    attention, back_q, back_v, grad_uq, grad_uv = pl.pallas_call(
        lambda *refs: attention_kernel(sizes, *refs),
        out_shape=(
            shape(rows, width),
            shape(rank, rows, dtype=F32),
            shape(members, rank, rows),
            shape(rank, width, dtype=F32),
            shape(rank, HD, dtype=F32),
        ),
        in_specs=[vmem] * 8,
        out_specs=(vmem,) * 5,
        scratch_shapes=[
            pltpu.VMEM((heads * rows, HD), BF16),
            pltpu.VMEM((heads * rows, HD), BF16),
            pltpu.VMEM((members, rows, HD), BF16),
            pltpu.VMEM((heads * rows, GROUP), F32),
            pltpu.VMEM((heads * rows, GROUP), BF16),
            pltpu.VMEM((heads * rows, HD), F32),
            pltpu.VMEM((heads * rows, HD), F32),
            pltpu.VMEM((heads * rows, HD), F32),
            pltpu.VMEM((heads * rows, HD), F32),
            pltpu.VMEM((HD, heads * rows), BF16),
            pltpu.VMEM((members, HD, rows), BF16),
        ],
        name="attention",
    )(low, keys, frozen_v, lowv, frozen_query, query_upper_factor, value_upper_factor, grad_output)

    down_q, down_v, upper_q, upper_v = pl.pallas_call(
        lambda *refs: reduce_kernel(sizes, *refs),
        out_shape=(
            shape(rank, width, dtype=F32),
            shape(rank, width, dtype=F32),
            shape(rank, width, dtype=F32),
            shape(rank, HD, dtype=F32),
        ),
        in_specs=[vmem] * 5,
        out_specs=(vmem,) * 4,
        scratch_shapes=[
            pltpu.VMEM((members, rank, rows), BF16),
            pltpu.VMEM((rank, rows), F32),
            pltpu.VMEM((count, 2 * rank, rows), BF16),
            pltpu.VMEM((chunks, rank, 128), BF16),
            pltpu.VMEM((seq_count, rank, 128), BF16),
            pltpu.VMEM((chunks, rank, 128), BF16),
            dma((members,)),
            dma((members,)),
            dma((count,)),
            dma((count,)),
            dma((seq_count,)),
            dma((seq_count,)),
            dma((seq_count,)),
            dma((seq_count,)),
        ],
        compiler_params=pltpu.CompilerParams(collective_id=1, has_side_effects=True),
        name="reduce",
    )(hidden_in, back_q, back_v, grad_uq, grad_uv)
    return (attention, down_q.T, upper_q, down_v.T, upper_v)


def solution(mesh):
    placed = (
        P("seq", "tensor"),
        P("seq", "tensor"),
        P("seq", "tensor"),
        P("seq", "tensor"),
        P("tensor", None),
        P(None, "tensor"),
        P("tensor", None),
        P(None, "tensor"),
        P("seq", "tensor"),
    )
    return jax.shard_map(
        per_device,
        mesh=mesh,
        in_specs=placed,
        out_specs=(
            P("seq", "tensor"),
            P("tensor", None),
            P(None, "tensor"),
            P("tensor", None),
            P(None, "tensor"),
        ),
        check_vma=False,
    )
```
